32 devices in a mesh: shot: 8 (over z, x), lag: 4 (over y, core).
Axes of the slice: x: 2, y: 2, z: 4, core: 2. Of those that a mesh axis runs over, the one named last changes fastest.
Arguments:
- traces: bfloat16 [48, 256, 8192], P('shot', 'lag'), may hold values from -64 to 64, as said below
- live_mask: int32 [48, 256], P('shot', 'lag'), may hold values 0 or 1
- gap_samples: int32 [1], replicated, may hold values from 1 to 32
Outputs:
- residual_traces: bfloat16 [48, 256, 8192], P('shot', 'lag')
The draws below stay inside these ranges and needn't reach their ends.
Inputs may be any that keep to these rules, and one draw needn't show every extreme that they name: `traces`: recorded samples.
All inputs are finite; a program needn't handle non-finite values. No bound on the sum of `live_mask` on one device may be relied on, other than what follows from the above.
Results may differ from the reference program's by a relative error of at most 0.015.
The reference program's roundings to bfloat16 on the way (of `table`, `spectra`, `rotated`, `filter_bf` and `error`) count: a program that leaves them out, or rounds other values in their place, can miss the bound.
Values may be sent and summed in bfloat16 or wider, within the bound.
A program may use at most 128 MiB of HBM per device.

```python
import jax
import jax.numpy as jnp
from jax import lax

CHANNELS = 256
SAMPLES = 8192
LAGS = 4
FREQS = 512
CORR_LAGS = 8
SHOTS = 48


def draw_traces(key, part):
    subkeys = jax.random.split(jax.random.fold_in(key, 7), 8)
    source_count = 128
    noise_part = 0.3 * jax.random.normal(subkeys[0], (SHOTS, CHANNELS, SAMPLES), jnp.float32)
    band_edge = jnp.pi * FREQS / SAMPLES
    centre = band_edge * jax.random.uniform(subkeys[1], (source_count,), jnp.float32, 0.15, 0.95)
    radius = jax.random.uniform(subkeys[2], (source_count,), jnp.float32, 0.96, 0.995)
    first_coef = 2.0 * radius * jnp.cos(centre)
    second_coef = -radius * radius
    variance = (1.0 + radius * radius) / ((1.0 - radius * radius) * ((1.0 + radius * radius) ** 2 - first_coef * first_coef))
    drive_scale = 1.0 / jnp.sqrt(variance)

    def advance(carry, sample_idx):
        earlier, latest = carry
        innovation = jax.random.normal(jax.random.fold_in(subkeys[3], sample_idx), (SHOTS, source_count), jnp.float32)
        updated = first_coef * latest + second_coef * earlier + drive_scale * innovation
        return ((latest, updated), updated)
    start_state = (jnp.zeros((SHOTS, source_count), jnp.float32), jnp.zeros((SHOTS, source_count), jnp.float32))
    final_state, sources = lax.scan(advance, start_state, jnp.arange(SAMPLES, dtype=jnp.int32))
    amplitude = jnp.exp(-3.0 * jnp.log(10.0) * jax.random.uniform(subkeys[4], (source_count,), jnp.float32))
    mixing = jax.random.normal(subkeys[5], (CHANNELS, source_count), jnp.float32) * (0.3 * amplitude)[None, :]
    shot_ramp = 3.0 ** (jnp.arange(SHOTS, dtype=jnp.float32) / max(SHOTS - 1, 1))
    chan_scale = jnp.exp(jax.random.uniform(subkeys[6], (CHANNELS,), jnp.float32, jnp.log(0.5), jnp.log(5.0)))
    trace_scale = jax.random.uniform(subkeys[7], (SHOTS, CHANNELS), jnp.float32, 0.7, 1.3) * chan_scale[None, :]
    coherent = jnp.einsum('tsm,cm->sct', sources, mixing)
    recorded = (noise_part + coherent) * trace_scale[:, :, None] * shot_ramp[:, None, None]
    return jnp.clip(recorded, -64.0, 64.0).astype(jnp.bfloat16)


def set_ends(result, stream_key, low, largest):
    longest = result.shape.index(max(result.shape))
    spots = []
    for shift in (0, 1):
        where = [jax.random.randint(jax.random.fold_in(stream_key, axis), (), 0, length) for axis, length in enumerate(result.shape)]
        where[longest] = (where[longest] + shift) % result.shape[longest]
        spots.append(tuple(where))
    return result.at[spots[0]].set(low).at[spots[1]].set(largest)


def setup_inputs(seed: int = 0) -> dict:
    arg_keys = jax.random.split(jax.random.key(seed), 4)
    traces = draw_traces(jax.random.fold_in(arg_keys[3], 71), 0)
    live_mask = set_ends((jax.random.randint(arg_keys[1], (SHOTS, CHANNELS), 0, 8) < 7).astype(jnp.int32), jax.random.fold_in(arg_keys[1], 1), 0, 1)
    gap_samples = jax.random.randint(arg_keys[2], (1,), 1, 33).astype(jnp.int32)
    return {"traces": traces, "live_mask": live_mask, "gap_samples": gap_samples}


def dft_table(first_row, row_count, samples, band_size):
    times_idx = jnp.arange(row_count, dtype=jnp.int32) + first_row
    harmonic = jnp.arange(1, band_size + 1, dtype=jnp.int32)
    phase = times_idx[:, None] * harmonic[None, :] % (2 * samples)
    angle = phase.astype(jnp.float32) * (jnp.pi / samples)
    return jnp.concatenate([jnp.cos(angle), jnp.sin(angle)], axis=1).astype(jnp.bfloat16)

def delay_tables(delays, samples, band_size):
    harmonic = jnp.arange(1, band_size + 1, dtype=jnp.int32)
    phase = delays[:, None] * harmonic[None, :] % (2 * samples)
    angle = phase.astype(jnp.float32) * (jnp.pi / samples)
    return (jnp.cos(angle), jnp.sin(angle))

def delay_apply(spectrum, cosine, sine):
    band_size = cosine.shape[-1]
    real_part = spectrum[..., :band_size]
    imag_part = spectrum[..., band_size:]
    return jnp.concatenate([real_part * cosine - imag_part * sine, imag_part * cosine + real_part * sine], axis=-1)

def reference(traces, live_mask, gap_samples):
    table = dft_table(0, SAMPLES, SAMPLES, FREQS)
    spacing = SAMPLES // (2 * FREQS)
    tap_delays = jnp.arange(LAGS, dtype=jnp.int32) * spacing
    lag_list = jnp.concatenate([tap_delays, gap_samples[0].astype(jnp.int32) + tap_delays])
    cosine, sine = delay_tables(lag_list, SAMPLES, FREQS)
    live_bf = live_mask.astype(jnp.bfloat16)

    def spectrum_of(shot_idx):
        masked = traces[shot_idx] * live_bf[shot_idx][:, None]
        return jnp.dot(masked.astype(jnp.float32), table.astype(jnp.float32), preferred_element_type=jnp.float32).astype(jnp.bfloat16)
    spectra = lax.map(spectrum_of, jnp.arange(SHOTS, dtype=jnp.int32))

    def accumulate(carry, spectrum):
        rotated = delay_apply(spectrum.astype(jnp.float32)[None], cosine[:, None, :], sine[:, None, :]).astype(jnp.bfloat16)
        update = jnp.einsum('kaf,bf->kab', rotated.astype(jnp.float32), spectrum.astype(jnp.float32))
        return (carry + update, None)
    start_sum = jnp.zeros((CORR_LAGS, CHANNELS, CHANNELS), jnp.float32)
    summed, unused = lax.scan(accumulate, start_sum, spectra)
    correlation = summed * (1.0 / SAMPLES) * (1.0 / (SAMPLES * SHOTS))
    whiten = 0.1 * jnp.mean(jnp.diagonal(correlation[0])) + 1e-06
    zero_lag = correlation[0] + whiten * jnp.eye(CHANNELS, dtype=jnp.float32)
    weighted = jnp.concatenate([zero_lag[None], correlation[1:]], axis=0)
    blocks = []
    for row_block in range(LAGS):
        row_parts = []
        for col_block in range(LAGS):
            if row_block >= col_block:
                row_parts.append(weighted[row_block - col_block])
            else:
                row_parts.append(weighted[col_block - row_block].T)
        blocks.append(jnp.concatenate(row_parts, axis=1))
    system = jnp.concatenate(blocks, axis=0)
    rhs = jnp.concatenate([weighted[LAGS + row_block] for row_block in range(LAGS)], axis=0)
    lower_factor = jnp.linalg.cholesky(system)
    filter_all = jax.scipy.linalg.cho_solve((lower_factor, True), rhs)
    filter_bf = filter_all.astype(jnp.bfloat16).reshape(LAGS, CHANNELS, CHANNELS)

    def residual_of(shot_idx):
        spectrum = spectra[shot_idx]
        mixed = jnp.einsum('jab,af->jbf', filter_bf.astype(jnp.float32), spectrum.astype(jnp.float32))
        shifted = delay_apply(mixed, cosine[LAGS:, None, :], sine[LAGS:, None, :])
        error = (spectrum.astype(jnp.float32) - jnp.sum(shifted, axis=0)).astype(jnp.bfloat16)
        restored = jnp.dot(error.astype(jnp.float32), table.T.astype(jnp.float32), preferred_element_type=jnp.float32)
        return (restored * (1.0 / SAMPLES) * live_bf[shot_idx].astype(jnp.float32)[:, None]).astype(jnp.bfloat16)
    return lax.map(residual_of, jnp.arange(SHOTS, dtype=jnp.int32))
```

```python
import functools

import jax
import jax.numpy as jnp
from jax import lax
from jax.experimental import pallas as pl
from jax.experimental.pallas import tpu as pltpu
from jax.sharding import PartitionSpec as P

LAGS=4
HALF=128
PIVOTS=4

def mm(a, b, dims=((1,), (0,))):
    return lax.dot_general(a, b, (dims, ((), ())), precision=lax.Precision.HIGHEST, preferred_element_type=jnp.float32)


def factor_half(mat):
    lane = lax.broadcasted_iota(jnp.int32, (8, HALF), 1)
    row = lax.broadcasted_iota(jnp.int32, (8, HALF), 0)
    count = HALF // 8
    tiles = [mat[8 * t : 8 * t + 8, :] for t in range(count)]

    def spread(x):
        return jnp.broadcast_to(x, (8, HALF))

    def reduce_by(p, inv, x):
        done = []
        for j in range(PIVOTS):
            value = x[j]
            for i in range(j):
                value = value - p[i, j] * done[i]
            done.append(value * inv[j])
        return done

    for k in range(0, HALF, PIVOTS):
        home, off = k // 8, k % 8
        rows = [spread(tiles[home][off + i : off + i + 1, :]) for i in range(PIVOTS)]
        p = {(i, j): spread(rows[i][:, k + j : k + j + 1]) for i in range(PIVOTS) for j in range(i, PIVOTS)}
        inside = (lane >= k) & (lane < k + PIVOTS)
        rows = [jnp.where(inside, jnp.where(lane == k + i, 1.0, 0.0), rows[i]) for i in range(PIVOTS)]
        inv = []
        for i in range(PIVOTS):
            for m in range(i):
                for j in range(i, PIVOTS):
                    if m == i - 1:
                        p[i, j] = p[i, j] - p[m, i] * p[m, j]
            inv.append(lax.rsqrt(p[i, i]))
            for j in range(i + 1, PIVOTS):
                p[i, j] = p[i, j] * inv[i]
            for l in range(i + 2, PIVOTS):
                for j in range(l, PIVOTS):
                    p[l, j] = p[l, j] - p[i, l] * p[i, j]
        w = reduce_by(p, inv, rows)
        for t in range(home, count):
            if t == home and off + PIVOTS == 8:
                updated = tiles[t]
            else:
                c = reduce_by(p, inv, [spread(tiles[t][:, k + j : k + j + 1]) for j in range(PIVOTS)])
                kept = jnp.where(inside, 0.0, tiles[t])
                updated = kept - ((c[0] * w[0] + c[1] * w[1]) + (c[2] * w[2] + c[3] * w[3]))
            if t == home:
                updated = jnp.where(row < off, tiles[t], updated)
                for i in range(PIVOTS):
                    updated = jnp.where(row == off + i, w[i], updated)
            tiles[t] = updated
    return jnp.concatenate(
        [jnp.where(lane <= row + 8 * t, tiles[t], 0.0) for t in range(count)], axis=0
    )


def solve_kernel(scales, corr_ref, rhs_ref, out_ref, aug, diag, first_inv, coupling):
    channels = corr_ref.shape[1]
    order = LAGS * channels
    width = aug.shape[1]
    block = 2 * HALF
    count = order // block
    local = rhs_ref.shape[-1]

    def scaled(x):
        return x * scales[0] * scales[1]

    for lag in range(LAGS):
        value = scaled(corr_ref[lag])
        if lag == 0:
            same = lax.broadcasted_iota(jnp.int32, value.shape, 0) == lax.broadcasted_iota(jnp.int32, value.shape, 1)
            trace = jnp.sum(jnp.where(same, value, 0.0))
            value = value + jnp.where(same, 0.1 * (trace / channels) + 1e-06, 0.0)
        else:
            flipped = value.T
        for low in range(LAGS - lag):
            high = low + lag
            rows, cols = low * channels, high * channels
            aug[rows : rows + channels, cols : cols + channels] = value if lag == 0 else flipped
    aug[:, order:] = jnp.zeros((order, width - order), jnp.float32)
    for tap in range(LAGS):
        aug[tap * channels : (tap + 1) * channels, order : order + local] = scaled(rhs_ref[tap])
    diag[...] = aug[:HALF, :HALF]

    def step(half_step, carry):
        diag[...] = factor_half(diag[...])
        for b in range(count):
            o = b * block
            mid, end = o + HALF, o + block

            @pl.when(half_step == 2 * b)
            def _():
                low = mm(aug[mid:end, o:mid], diag[...], ((1,), (1,)))
                first_inv[...] = diag[...]
                coupling[...] = low
                diag[...] = aug[mid:end, mid:end] - mm(low, low, ((1,), (1,)))

            @pl.when(half_step == 2 * b + 1)
            def _():
                top, last = first_inv[...], diag[...]
                corner = -mm(last, mm(coupling[...], top))
                aug[o:mid, o:mid] = top
                aug[o:mid, mid:end] = jnp.zeros((HALF, HALF), jnp.float32)
                aug[mid:end, o:mid] = corner
                aug[mid:end, mid:end] = last
                for c in range(end, width, block):
                    ce = min(c + block, width)
                    aug[o:end, c:ce] = mm(aug[o:end, o:end], aug[o:end, c:ce])
                for r in range(end, order, block):
                    left = aug[o:end, r : r + block]
                    for c in range(r, width, block):
                        ce = min(c + block, width)
                        aug[r : r + block, c:ce] = aug[r : r + block, c:ce] - mm(left, aug[o:end, c:ce], ((0,), (0,)))
                if end < order:
                    diag[...] = aug[end : end + HALF, end : end + HALF]

        return carry

    lax.fori_loop(0, 2 * count, step, 0)
    for b in range(count - 1, -1, -1):
        o, end = b * block, (b + 1) * block
        known = aug[o:end, order:]
        if end < order:
            known = known - mm(aug[o:end, end:order], aug[end:order, order:])
        aug[o:end, order:] = mm(aug[o:end, o:end], known, ((0,), (0,)))
    out_ref[...] = aug[:, order : order + local].astype(jnp.bfloat16)


def solve(corr, rhs, scales):
    channels = corr.shape[1]
    local = rhs.shape[-1]
    order = LAGS * channels
    width = order + HALF * pl.cdiv(local, HALF)
    vm = pl.BlockSpec(memory_space=pltpu.VMEM)
    return pl.pallas_call(
        functools.partial(solve_kernel, scales),
        out_shape=jax.ShapeDtypeStruct((order, local), jnp.bfloat16),
        in_specs=[vm, vm],
        out_specs=vm,
        scratch_shapes=[
            pltpu.VMEM((order, width), jnp.float32),
            pltpu.VMEM((HALF, HALF), jnp.float32),
            pltpu.VMEM((HALF, HALF), jnp.float32),
            pltpu.VMEM((HALF, HALF), jnp.float32),
        ],
        compiler_params=pltpu.CompilerParams(vmem_limit_bytes=40 << 20),
        name="block_solve",
    )(corr, rhs)


def dft_table(samples, band_size):
    fine_count = 1
    while fine_count * fine_count < samples:
        fine_count *= 2
    harmonic = jnp.arange(1, band_size + 1, dtype=jnp.int32)

    def circle(times):
        phase = times[:, None] * harmonic[None, :] % (2 * samples)
        angle = phase.astype(jnp.float32) * (jnp.pi / samples)
        return jnp.cos(angle), jnp.sin(angle)

    fine_cos, fine_sin = circle(jnp.arange(fine_count, dtype=jnp.int32))
    coarse_cos, coarse_sin = circle(jnp.arange(samples // fine_count, dtype=jnp.int32) * fine_count)
    first = jnp.concatenate([coarse_cos, coarse_sin], axis=1)[:, None, :]
    second = jnp.concatenate([-coarse_sin, coarse_cos], axis=1)[:, None, :]
    cosines = jnp.concatenate([fine_cos, fine_cos], axis=1)[None]
    sines = jnp.concatenate([fine_sin, fine_sin], axis=1)[None]
    table = (first * cosines + second * sines).astype(jnp.bfloat16)
    return table.reshape(samples, 2 * band_size)


def delay_tables(delays, samples, band_size):
    harmonic = jnp.arange(1, band_size + 1, dtype=jnp.int32)
    phase = delays[:, None] * harmonic[None, :] % (2 * samples)
    angle = phase.astype(jnp.float32) * (jnp.pi / samples)
    return (jnp.cos(angle), jnp.sin(angle))


def delay_apply(spectrum, cosine, sine):
    band_size = cosine.shape[-1]
    real_part = spectrum[..., :band_size]
    imag_part = spectrum[..., band_size:]
    return jnp.concatenate(
        [real_part * cosine - imag_part * sine, imag_part * cosine + real_part * sine], axis=-1
    )


def shards(traces, live_mask, gap_samples):
    shot_count, local_chan, samples = traces.shape
    band_size = samples // 16
    shot_shards = lax.axis_size("shot")
    table = lax.optimization_barrier(dft_table(samples, band_size))
    live_float = live_mask.astype(jnp.float32)[:, :, None]
    running = jnp.einsum("sct,tw->scw", traces, table, preferred_element_type=jnp.float32)
    own_spec = (running * live_float).astype(jnp.bfloat16)
    all_spec = lax.all_gather(own_spec, "lag", axis=1, tiled=True)
    spacing = samples // (2 * band_size)
    tap_delays = jnp.arange(LAGS, dtype=jnp.int32) * spacing
    lag_list = jnp.concatenate([tap_delays, gap_samples[0] + tap_delays])
    cosine, sine = delay_tables(lag_list, samples, band_size)
    rotated = delay_apply(
        own_spec.astype(jnp.float32)[None], cosine[:, None, None, :], sine[:, None, None, :]
    ).astype(jnp.bfloat16)
    partial_value = jnp.einsum(
        "ksaf,sbf->kab", rotated, all_spec, preferred_element_type=jnp.float32
    )
    channels = all_spec.shape[1]
    pieces = partial_value.reshape(shot_shards, -1, channels)
    pieces = lax.all_to_all(pieces, "shot", 0, 0, tiled=False)
    reduced = jnp.sum(pieces, axis=0)
    summed = lax.all_gather(reduced, "shot", axis=0, tiled=True)
    summed = summed.reshape(2 * LAGS, local_chan, channels)
    gathered = lax.all_gather(summed, "lag", axis=1, tiled=True)
    first_out = lax.axis_index("lag") * local_chan
    rhs = lax.dynamic_slice(gathered, (LAGS, 0, first_out), (LAGS, channels, local_chan))
    total_shots = shot_count * shot_shards
    filter_own = solve(gathered[:LAGS], rhs, (1.0 / samples, 1.0 / (samples * total_shots)))
    filter_bf = filter_own.reshape(LAGS, channels, local_chan)
    mixed = jnp.einsum("jab,saf->jsbf", filter_bf, all_spec, preferred_element_type=jnp.float32)
    shifted = delay_apply(mixed, cosine[LAGS:, None, None, :], sine[LAGS:, None, None, :])
    predicted = jnp.sum(shifted, axis=0)
    error = (own_spec.astype(jnp.float32) - predicted).astype(jnp.bfloat16)
    restored = jnp.einsum("scw,tw->sct", error, table, preferred_element_type=jnp.float32)
    return (restored * (1.0 / samples) * live_float).astype(jnp.bfloat16)


def solution(mesh):
    placed = (P("shot", "lag", None), P("shot", "lag"), P())
    return jax.shard_map(
        shards, mesh=mesh, in_specs=placed, out_specs=P("shot", "lag", None), check_vma=False
    )
```

```python
import functools

import jax
import jax.numpy as jnp
from jax import lax
from jax.experimental import pallas as pl
from jax.experimental.pallas import tpu as pltpu
from jax.sharding import PartitionSpec as P

LAGS=4
HALF=128
PIVOTS=4

def mm(a, b, dims=((1,), (0,))):
    return lax.dot_general(a, b, (dims, ((), ())), precision=lax.Precision.HIGHEST, preferred_element_type=jnp.float32)


def factor_half(mat):
    lane = lax.broadcasted_iota(jnp.int32, (8, HALF), 1)
    row = lax.broadcasted_iota(jnp.int32, (8, HALF), 0)
    count = HALF // 8
    tiles = [mat[8 * t : 8 * t + 8, :] for t in range(count)]

    def spread(x):
        return jnp.broadcast_to(x, (8, HALF))

    def reduce_by(p, inv, x):
        done = []
        for j in range(PIVOTS):
            value = x[j]
            for i in range(j):
                value = value - p[i, j] * done[i]
            done.append(value * inv[j])
        return done

    for k in range(0, HALF, PIVOTS):
        home, off = k // 8, k % 8
        rows = [spread(tiles[home][off + i : off + i + 1, :]) for i in range(PIVOTS)]
        p = {(i, j): spread(rows[i][:, k + j : k + j + 1]) for i in range(PIVOTS) for j in range(i, PIVOTS)}
        inside = (lane >= k) & (lane < k + PIVOTS)
        rows = [jnp.where(inside, jnp.where(lane == k + i, 1.0, 0.0), rows[i]) for i in range(PIVOTS)]
        inv = []
        for i in range(PIVOTS):
            for m in range(i):
                for j in range(i, PIVOTS):
                    if m == i - 1:
                        p[i, j] = p[i, j] - p[m, i] * p[m, j]
            inv.append(lax.rsqrt(p[i, i]))
            for j in range(i + 1, PIVOTS):
                p[i, j] = p[i, j] * inv[i]
            for l in range(i + 2, PIVOTS):
                for j in range(l, PIVOTS):
                    p[l, j] = p[l, j] - p[i, l] * p[i, j]
        w = reduce_by(p, inv, rows)
        for t in range(home, count):
            if t == home and off + PIVOTS == 8:
                updated = tiles[t]
            else:
                c = reduce_by(p, inv, [spread(tiles[t][:, k + j : k + j + 1]) for j in range(PIVOTS)])
                kept = jnp.where(inside, 0.0, tiles[t])
                updated = kept - ((c[0] * w[0] + c[1] * w[1]) + (c[2] * w[2] + c[3] * w[3]))
            if t == home:
                updated = jnp.where(row < off, tiles[t], updated)
                for i in range(PIVOTS):
                    updated = jnp.where(row == off + i, w[i], updated)
            tiles[t] = updated
    return jnp.concatenate(
        [jnp.where(lane <= row + 8 * t, tiles[t], 0.0) for t in range(count)], axis=0
    )


def solve_kernel(scales, corr_ref, rhs_ref, out_ref, aug, diag, first_inv, coupling):
    channels = corr_ref.shape[1]
    order = LAGS * channels
    width = aug.shape[1]
    block = 2 * HALF
    count = order // block
    local = rhs_ref.shape[-1]

    def scaled(x):
        return x * scales[0] * scales[1]

    for lag in range(LAGS):
        value = scaled(corr_ref[lag])
        if lag == 0:
            same = lax.broadcasted_iota(jnp.int32, value.shape, 0) == lax.broadcasted_iota(jnp.int32, value.shape, 1)
            trace = jnp.sum(jnp.where(same, value, 0.0))
            value = value + jnp.where(same, 0.1 * (trace / channels) + 1e-06, 0.0)
        else:
            flipped = value.T
        for low in range(LAGS - lag):
            high = low + lag
            rows, cols = low * channels, high * channels
            aug[rows : rows + channels, cols : cols + channels] = value if lag == 0 else flipped
    aug[:, order:] = jnp.zeros((order, width - order), jnp.float32)
    for tap in range(LAGS):
        aug[tap * channels : (tap + 1) * channels, order : order + local] = scaled(rhs_ref[tap])
    diag[...] = aug[:HALF, :HALF]

    def step(half_step, carry):
        diag[...] = factor_half(diag[...])
        for b in range(count):
            o = b * block
            mid, end = o + HALF, o + block

            @pl.when(half_step == 2 * b)
            def _():
                low = mm(aug[mid:end, o:mid], diag[...], ((1,), (1,)))
                first_inv[...] = diag[...]
                coupling[...] = low
                diag[...] = aug[mid:end, mid:end] - mm(low, low, ((1,), (1,)))

            @pl.when(half_step == 2 * b + 1)
            def _():
                top, last = first_inv[...], diag[...]
                corner = -mm(last, mm(coupling[...], top))
                aug[o:mid, o:mid] = top
                aug[o:mid, mid:end] = jnp.zeros((HALF, HALF), jnp.float32)
                aug[mid:end, o:mid] = corner
                aug[mid:end, mid:end] = last
                for c in range(end, width, block):
                    ce = min(c + block, width)
                    aug[o:end, c:ce] = mm(aug[o:end, o:end], aug[o:end, c:ce])
                for r in range(end, order, block):
                    left = aug[o:end, r : r + block]
                    for c in range(r, width, block):
                        ce = min(c + block, width)
                        aug[r : r + block, c:ce] = aug[r : r + block, c:ce] - mm(left, aug[o:end, c:ce], ((0,), (0,)))
                if end < order:
                    diag[...] = aug[end : end + HALF, end : end + HALF]

        return carry

    lax.fori_loop(0, 2 * count, step, 0)
    for b in range(count - 1, -1, -1):
        o, end = b * block, (b + 1) * block
        known = aug[o:end, order:]
        if end < order:
            known = known - mm(aug[o:end, end:order], aug[end:order, order:])
        aug[o:end, order:] = mm(aug[o:end, o:end], known, ((0,), (0,)))
    out_ref[...] = aug[:, order : order + local].astype(jnp.bfloat16)


def solve(corr, rhs, scales):
    channels = corr.shape[1]
    local = rhs.shape[-1]
    order = LAGS * channels
    width = order + HALF * pl.cdiv(local, HALF)
    vm = pl.BlockSpec(memory_space=pltpu.VMEM)
    return pl.pallas_call(
        functools.partial(solve_kernel, scales),
        out_shape=jax.ShapeDtypeStruct((order, local), jnp.bfloat16),
        in_specs=[vm, vm],
        out_specs=vm,
        scratch_shapes=[
            pltpu.VMEM((order, width), jnp.float32),
            pltpu.VMEM((HALF, HALF), jnp.float32),
            pltpu.VMEM((HALF, HALF), jnp.float32),
            pltpu.VMEM((HALF, HALF), jnp.float32),
        ],
        compiler_params=pltpu.CompilerParams(vmem_limit_bytes=40 << 20),
        name="block_solve",
    )(corr, rhs)


def dft_table(samples, band_size):
    fine_count = 1
    while fine_count * fine_count < samples:
        fine_count *= 2
    harmonic = jnp.arange(1, band_size + 1, dtype=jnp.int32)

    def circle(times):
        phase = times[:, None] * harmonic[None, :] % (2 * samples)
        angle = phase.astype(jnp.float32) * (jnp.pi / samples)
        return jnp.cos(angle), jnp.sin(angle)

    fine_cos, fine_sin = circle(jnp.arange(fine_count, dtype=jnp.int32))
    coarse_cos, coarse_sin = circle(jnp.arange(samples // fine_count, dtype=jnp.int32) * fine_count)
    first = jnp.concatenate([coarse_cos, coarse_sin], axis=1)[:, None, :]
    second = jnp.concatenate([-coarse_sin, coarse_cos], axis=1)[:, None, :]
    cosines = jnp.concatenate([fine_cos, fine_cos], axis=1)[None]
    sines = jnp.concatenate([fine_sin, fine_sin], axis=1)[None]
    table = (first * cosines + second * sines).astype(jnp.bfloat16)
    return table.reshape(samples, 2 * band_size)


def restore_kernel(scale, error_ref, table_ref, live_ref, out_ref):
    value = lax.dot_general(
        error_ref[...], table_ref[...], (((1,), (1,)), ((), ())), preferred_element_type=jnp.float32
    )
    out_ref[...] = (value * scale * live_ref[...]).astype(jnp.bfloat16)


def restore(error, table, live):
    rows, depth = error.shape
    samples = table.shape[0]
    step = min(1024, samples)
    return pl.pallas_call(
        functools.partial(restore_kernel, 1.0 / samples),
        out_shape=jax.ShapeDtypeStruct((rows, samples), jnp.bfloat16),
        grid=(samples // step,),
        in_specs=[
            pl.BlockSpec((rows, depth), lambda t: (0, 0)),
            pl.BlockSpec((step, depth), lambda t: (t, 0)),
            pl.BlockSpec((rows, 1), lambda t: (0, 0)),
        ],
        out_specs=pl.BlockSpec((rows, step), lambda t: (0, t)),
        compiler_params=pltpu.CompilerParams(vmem_limit_bytes=24 << 20),
        name="restore",
    )(error, table, live)


def delay_tables(delays, samples, band_size):
    harmonic = jnp.arange(1, band_size + 1, dtype=jnp.int32)
    phase = delays[:, None] * harmonic[None, :] % (2 * samples)
    angle = phase.astype(jnp.float32) * (jnp.pi / samples)
    return (jnp.cos(angle), jnp.sin(angle))


def delay_apply(spectrum, cosine, sine):
    band_size = cosine.shape[-1]
    real_part = spectrum[..., :band_size]
    imag_part = spectrum[..., band_size:]
    return jnp.concatenate(
        [real_part * cosine - imag_part * sine, imag_part * cosine + real_part * sine], axis=-1
    )


def shards(traces, live_mask, gap_samples):
    shot_count, local_chan, samples = traces.shape
    band_size = samples // 16
    shot_shards = lax.axis_size("shot")
    table = lax.optimization_barrier(dft_table(samples, band_size))
    live_float = live_mask.astype(jnp.float32)[:, :, None]
    running = jnp.einsum("sct,tw->scw", traces, table, preferred_element_type=jnp.float32)
    own_spec = (running * live_float).astype(jnp.bfloat16)
    all_spec = lax.all_gather(own_spec, "lag", axis=1, tiled=True)
    spacing = samples // (2 * band_size)
    tap_delays = jnp.arange(LAGS, dtype=jnp.int32) * spacing
    lag_list = jnp.concatenate([tap_delays, gap_samples[0] + tap_delays])
    cosine, sine = delay_tables(lag_list, samples, band_size)
    rotated = delay_apply(
        own_spec.astype(jnp.float32)[None], cosine[:, None, None, :], sine[:, None, None, :]
    ).astype(jnp.bfloat16)
    partial_value = jnp.einsum(
        "ksaf,sbf->kab", rotated, all_spec, preferred_element_type=jnp.float32
    )
    channels = all_spec.shape[1]
    pieces = partial_value.reshape(shot_shards, -1, channels)
    pieces = lax.all_to_all(pieces, "shot", 0, 0, tiled=False)
    reduced = jnp.sum(pieces, axis=0)
    copies = jnp.broadcast_to(reduced[None], (shot_shards,) + reduced.shape)
    summed = lax.all_to_all(copies, "shot", 0, 0, tiled=False)
    summed = summed.reshape(2 * LAGS, local_chan, channels)
    gathered = lax.all_gather(summed, "lag", axis=1, tiled=True)
    first_out = lax.axis_index("lag") * local_chan
    rhs = lax.dynamic_slice(gathered, (LAGS, 0, first_out), (LAGS, channels, local_chan))
    total_shots = shot_count * shot_shards
    filter_own = solve(gathered[:LAGS], rhs, (1.0 / samples, 1.0 / (samples * total_shots)))
    filter_bf = filter_own.reshape(LAGS, channels, local_chan)
    mixed = jnp.einsum("jab,saf->jsbf", filter_bf, all_spec, preferred_element_type=jnp.float32)
    shifted = delay_apply(mixed, cosine[LAGS:, None, None, :], sine[LAGS:, None, None, :])
    predicted = jnp.sum(shifted, axis=0)
    error = (own_spec.astype(jnp.float32) - predicted).astype(jnp.bfloat16)
    rows = shot_count * local_chan
    restored = restore(error.reshape(rows, -1), table, live_float.reshape(rows, 1))
    return restored.reshape(shot_count, local_chan, samples)


def solution(mesh):
    placed = (P("shot", "lag", None), P("shot", "lag"), P())
    return jax.shard_map(
        shards, mesh=mesh, in_specs=placed, out_specs=P("shot", "lag", None), check_vma=False
    )
```
